256 devices in a mesh: blk: 32 (over x_hi, z, core), req: 8 (over y, x_lo).
Axes of the slice: x: 4 (x_hi: 2, x_lo: 2; x = x_hi * 2 + x_lo), y: 4, z: 8, core: 2. Of those that a mesh axis runs over, the one named last changes fastest.
Arguments:
- prefill_queries: bfloat16 [8, 512, 1024], P('req', 'blk'), may hold values from -6 to 6
- decode_queries: bfloat16 [128, 1024], P('req'), may hold values from -6 to 6
- new_prefill: bfloat16 [8, 512, 512], P('req', 'blk'), may hold values from -6 to 6
- new_decode: bfloat16 [128, 512], P('req'), may hold values from -6 to 6
- prefill_cache: bfloat16 [8, 4096, 512], P('req', 'blk'), may hold values from -5 to 5
- decode_cache: bfloat16 [128, 4096, 512], P('req', 'blk'), may hold values from -5 to 5
- prefill_offsets: int32 [8], P('req'), may hold values from 2 to 3584, as said below
- decode_lengths: int32 [128], P('req'), may hold values from 2 to 4095, as said below
- dealing: int32 [136], replicated, may hold values from 0 to 127, as said below
Outputs:
- prefill_out: bfloat16 [8, 512, 1024], P('req', 'blk')
- decode_out: bfloat16 [128, 1024], P('req')
- prefill_cache_out: bfloat16 [8, 4096, 512], P('req', 'blk')
- decode_cache_out: bfloat16 [128, 4096, 512], P('req', 'blk')
The draws below stay inside these ranges and needn't reach their ends.
Inputs may be any that keep to these rules, and one draw needn't show every extreme that they name: The block of prefill slot i fills positions prefill_offsets[i] to prefill_offsets[i] + 511; some slot has offset 4096 - 512. The new token of decode slot j goes to position decode_lengths[j]; some slot has length 4095. `dealing`: the first 8 entries are a permutation of 0 to 7, the other 128 a permutation of 0 to 127.
All inputs are finite; a program needn't handle non-finite values.
Results may differ from the reference program's by a relative error of at most 0.0085.
Values may be sent and summed in bfloat16 or wider, within the bound.
A program may use at most 64 MiB of HBM per device.

```python
import jax
import jax.numpy as jnp
from jax import lax

QUERY_HEADS = 8
KEY_VALUE_HEADS = 2
HEAD_SIZE = 128
P_SIZE = 512
KVW = 512
CTX = 4096
NPRE = 8
NDEC = 128


def cache_draw(key, slots, salt):
    drawn = jax.random.truncated_normal(jax.random.fold_in(key, salt + 1), -4.0, 4.0, (slots, CTX, KVW), jnp.float32)
    return drawn.astype(jnp.bfloat16)


def draw_prefill_cache(key, part):
    return cache_draw(key, NPRE, 7)


def draw_decode_cache(key, part):
    return cache_draw(key, NDEC, 11)


def draw_prefill_queries(key, part):
    drawn = 2.0 * jax.random.truncated_normal(jax.random.fold_in(key, 31), -3.0, 3.0, (NPRE, P_SIZE, QUERY_HEADS * HEAD_SIZE), jnp.float32)
    return drawn.astype(jnp.bfloat16)


def draw_decode_queries(key, part):
    drawn = 2.0 * jax.random.truncated_normal(jax.random.fold_in(key, 33), -3.0, 3.0, (NDEC, QUERY_HEADS * HEAD_SIZE), jnp.float32)
    return drawn.astype(jnp.bfloat16)


def skewed_positions(key, count, upper, salt):
    first_draw = jax.random.randint(jax.random.fold_in(key, salt), (count,), 0, upper - 1)
    second_draw = jax.random.randint(jax.random.fold_in(key, salt + 1), (count,), 0, upper - 1)
    skewed = 2 + first_draw * second_draw // upper
    longest = jax.random.randint(jax.random.fold_in(key, salt + 2), (), 0, count)
    slots = jnp.arange(count)
    skewed = jnp.where(slots == longest, upper, skewed)
    return skewed.astype(jnp.int32)


def draw_prefill_offsets(key, part):
    return skewed_positions(key, NPRE, CTX - P_SIZE, 41)


def draw_decode_lengths(key, part):
    return skewed_positions(key, NDEC, CTX - 1, 45)


def draw_dealing(key, part):
    first_order = jax.random.permutation(jax.random.fold_in(key, 51), NPRE)
    second_order = jax.random.permutation(jax.random.fold_in(key, 52), NDEC)
    return jnp.concatenate([first_order, second_order]).astype(jnp.int32)


def block_levels(stream_key, dims, cuts, low, top_value):
    def one(position, blocks):
        draws = jax.random.uniform(jax.random.fold_in(jax.random.fold_in(stream_key, 6), position), (blocks,), jnp.float32, low / len(cuts), top_value / len(cuts))
        return jnp.repeat(jnp.exp(draws), dims[position] // blocks).reshape((-1,) + (1,) * (len(dims) - position - 1))

    factor_of = one(*cuts[0])
    for cut in cuts[1:]:
        factor_of = factor_of * one(*cut)
    return factor_of


def centred(stream_key, extent, scale, limit, shards=(), kind=jnp.bfloat16):
    factor_of = block_levels(stream_key, extent, shards, -0.22, 0.18) if shards else 1.0
    result = jax.random.normal(stream_key, extent, jnp.float32) * scale * factor_of
    return jnp.minimum(jnp.maximum(result, -limit), limit).astype(kind)


def setup_inputs(seed: int = 0) -> dict:
    streams_of = jax.random.split(jax.random.key(seed), 10)
    return {
        "prefill_queries": draw_prefill_queries(jax.random.fold_in(streams_of[9], 71), 0),
        "decode_queries": draw_decode_queries(jax.random.fold_in(streams_of[9], 71), 0),
        "new_prefill": centred(streams_of[2], (NPRE, P_SIZE, KVW), 1.0, 6.0, ((0, 8), (1, 32))),
        "new_decode": centred(streams_of[3], (NDEC, KVW), 1.0, 6.0, ((0, 8),)),
        "prefill_cache": draw_prefill_cache(jax.random.fold_in(streams_of[9], 71), 0),
        "decode_cache": draw_decode_cache(jax.random.fold_in(streams_of[9], 71), 0),
        "prefill_offsets": draw_prefill_offsets(jax.random.fold_in(streams_of[9], 71), 0),
        "decode_lengths": draw_decode_lengths(jax.random.fold_in(streams_of[9], 71), 0),
        "dealing": draw_dealing(jax.random.fold_in(streams_of[9], 71), 0),
    }


masked_fill = -1e30


def heads_attend(query_rows, cache_table, limits):
    row_total = query_rows.shape[0]
    grouped_queries = query_rows.astype(jnp.float32).reshape(row_total, KEY_VALUE_HEADS, QUERY_HEADS // KEY_VALUE_HEADS, HEAD_SIZE)
    key_portion = cache_table[:, :KEY_VALUE_HEADS * HEAD_SIZE].astype(jnp.float32).reshape(-1, KEY_VALUE_HEADS, HEAD_SIZE)
    value_portion = cache_table[:, KEY_VALUE_HEADS * HEAD_SIZE:].astype(jnp.float32).reshape(-1, KEY_VALUE_HEADS, HEAD_SIZE)
    scores = jnp.einsum("rgqd,cgd->gqrc", grouped_queries, key_portion) * (HEAD_SIZE ** -0.5)
    visible = jnp.arange(cache_table.shape[0], dtype=jnp.int32)[None, :] <= limits[:, None]
    scores = jnp.where(visible, scores, masked_fill)
    maxima = jnp.max(scores, axis=-1, keepdims=True)
    exponent = jnp.where(visible, jnp.exp(scores - maxima), 0.0)
    totals = jnp.sum(exponent, axis=-1)
    rounded = lax.optimization_barrier(exponent.astype(jnp.bfloat16)).astype(jnp.float32)
    weighted = jnp.einsum("gqrc,cgd->gqrd", rounded, value_portion)
    normed = weighted / totals[..., None]
    return jnp.transpose(normed, (2, 0, 1, 3)).reshape(row_total, QUERY_HEADS * HEAD_SIZE).astype(jnp.bfloat16)


def reference(prefill_queries, decode_queries, new_prefill, new_decode, prefill_cache, decode_cache, prefill_offsets, decode_lengths, dealing):
    positions = jnp.arange(CTX, dtype=jnp.int32)
    relative = positions[None, :] - prefill_offsets[:, None]
    picked = jax.vmap(lambda source_rows, row_index: source_rows[row_index])(new_prefill, jnp.clip(relative, 0, P_SIZE - 1).astype(jnp.int32))
    inside = (relative >= 0) & (relative < P_SIZE)
    prefill_cache_out = jnp.where(inside[:, :, None], picked, prefill_cache)
    written = positions[None, :] == decode_lengths[:, None]
    decode_cache_out = jnp.where(written[:, :, None], new_decode[:, None, :], decode_cache)
    prefill_limits = prefill_offsets[:, None] + jnp.arange(P_SIZE, dtype=jnp.int32)[None, :]
    prefill_attn = lax.map(lambda operands: heads_attend(operands[0], operands[1], operands[2]), (prefill_queries, prefill_cache_out, prefill_limits))
    decode_attn = lax.map(lambda operands: heads_attend(operands[0], operands[1], operands[2]), (decode_queries[:, None, :], decode_cache_out, decode_lengths[:, None]))
    decode_attn = decode_attn.reshape(NDEC, QUERY_HEADS * HEAD_SIZE)
    prefill_out = jnp.zeros_like(prefill_attn).at[dealing[:NPRE]].set(prefill_attn)
    decode_out = jnp.zeros_like(decode_attn).at[dealing[NPRE:]].set(decode_attn)
    return (prefill_out, decode_out, prefill_cache_out, decode_cache_out)
```

```python
import functools
import math

import jax
import jax.numpy as jnp
from jax import lax
from jax.experimental import pallas as pl
from jax.experimental.pallas import tpu as pltpu
from jax.sharding import PartitionSpec as P

HEADS = 8
D = 128
TOK = 16
ROWS = 128
SLOTS = 16
NEG = -1e30
LOG2E = math.log2(math.e)
SCALE2 = D ** (-0.5) * LOG2E
BIG = 1 << 24
BF = jnp.bfloat16
F32 = jnp.float32
I32 = jnp.int32
NT = (((1,), (1,)), ((), ()))
TN = (((0,), (0,)), ((), ()))


def iota(shape, axis):
    return lax.broadcasted_iota(I32, shape, axis)


def dot(a, b, dims):
    return lax.dot_general(a, b, dims, preferred_element_type=F32)


def soft(s):
    m = jnp.max(s, axis=0, keepdims=True)
    p = jnp.exp2((s - m) * SCALE2)
    total = jnp.sum(p, axis=0, keepdims=True)
    return p, total, m * SCALE2 + jnp.log(total) * LOG2E


def put(ref, rows, o, lse):
    ref[0:rows, :] = o.astype(BF)
    hi = lse.astype(BF).astype(F32)
    mid = (lse - hi).astype(BF).astype(F32)
    low = lse - hi - mid
    row = iota((16, 128), 0)
    tile = jnp.where(row == 0, hi, jnp.where(row == 1, mid, jnp.where(row == 2, low, 0.0)))
    ref[rows : rows + 16, :] = tile.astype(BF)


def get_lse(ref, rows):
    return jnp.sum(ref[rows : rows + 16, :].astype(F32), axis=0, keepdims=True)


def merge(refs, rows):
    lses = [get_lse(ref, rows) for ref in refs]
    top = functools.reduce(jnp.maximum, lses)
    weights = [jnp.exp2(x - top) for x in lses]
    total = functools.reduce(jnp.add, weights)
    inv = 1.0 / total
    out = None
    for ref, w in zip(refs, weights):
        term = ref[0:rows, :].astype(F32) * (w * inv)
        out = term if out is None else out + term
    return out, top + jnp.log(total) * LOG2E


def body(
    Z, Y,
    q, dq, new, pc, dcache, off, lens, deal,
    pout, dout, cout,
    kbuf, vbuf, keyval, qall, dbuf, dsend, d1, d3, rdq, df,
    psend, pall, nk, nv, sel, nx, rsend, rall,
    s_load, s_loc,
    s_kv, r_kv, s_q, r_q, s_p, r_p, s_n, r_n,
    s_d1, r_d1, s_d3, r_d3, s_rd, r_rd, s_df, r_df, s_nx, r_nx, s_r, r_r,
):
    b = lax.axis_index("blk")
    r = lax.axis_index("req")
    c = lax.rem(b, 2)
    z = lax.rem(b // 2, Z)
    xh = b // (2 * Z)
    xl = lax.rem(r, 2)
    y = r // 2
    NP = 2 * Y

    def blk_at(dx, dz, dc):
        return lax.rem(xh + dx, 2) * (2 * Z) + lax.rem(z + dz, Z) * 2 + lax.rem(c + dc, 2)

    def req_at(dy, dl):
        return lax.rem(y + dy, Y) * 2 + lax.rem(xl + dl, 2)

    def rcopy(src, dst, ss, rs, blk, req):
        return pltpu.make_async_remote_copy(
            src_ref=src, dst_ref=dst, send_sem=ss, recv_sem=rs,
            device_id={"blk": blk, "req": req}, device_id_type=pl.DeviceIdType.MESH,
        )

    plane = [(0, 1), (1, 0), (1, 1)]
    reqs = [(dy, dl) for dy in range(Y) for dl in range(2)]

    loads = []
    for i in range(4):
        cp = pltpu.make_async_copy(
            dcache.at[pl.ds(4 * i, 4)], dbuf.at[pl.ds(4 * i, 4)], s_load.at[i]
        )
        cp.start()
        loads.append(cp)

    barrier = pltpu.get_barrier_semaphore()
    partners = [(blk_at(dx, 0, dc), r) for dx, dc in plane]
    partners += [(blk_at(0, k, dc), r) for k in range(1, Z) for dc in range(2)]
    partners += [(blk_at(0, 0, dc), req_at(dy, dl)) for dy, dl in reqs[1:] for dc in range(2)]
    for blk, req in partners:
        pl.semaphore_signal(
            barrier, inc=1, device_id={"blk": blk, "req": req},
            device_id_type=pl.DeviceIdType.MESH,
        )

    lane = iota((1, 128), 1)
    lane_slot = lax.rem(lane, SLOTS)
    zero = jnp.zeros((SLOTS, D), BF)
    rows = []
    for h in range(HEADS):
        x = dq[:, h * D : (h + 1) * D]
        rows.append(jnp.concatenate([x, zero] if h < 4 else [zero, x], axis=1))
    qbd = jnp.concatenate(rows, axis=0)
    limit = jnp.zeros((1, 128), I32)
    for j in range(SLOTS):
        limit = jnp.where(lane_slot == j, lens[j], limit)
    sc = jnp.zeros((ROWS, 128), F32)
    for i in range(4):
        loads[i].wait()
        keys = dbuf[4 * i : 4 * i + 4, :, 0 : 2 * D].reshape(4 * ROWS, 2 * D)
        s = dot(keys, qbd, NT)
        for j in range(4):
            sc = jnp.where(lane_slot == 4 * i + j, s[j * ROWS : (j + 1) * ROWS], sc)
    pos = b * ROWS + iota((ROWS, 128), 0)
    p, total, lse = soft(jnp.where(pos <= limit, sc, NEG))
    p_t = jnp.transpose(p)
    row_slot = lax.rem(iota((128, 128), 0), SLOTS)
    p_all = jnp.concatenate(
        [jnp.where(row_slot == j, p_t, 0.0).astype(BF) for j in range(SLOTS)], axis=1
    )
    values = dbuf[:, :, 2 * D : 4 * D].reshape(SLOTS * ROWS, 2 * D)
    o = jnp.dot(p_all, values, preferred_element_type=F32)
    o = jnp.concatenate([o[0:64, 0:D], o[64:128, D : 2 * D]], axis=0)
    o_t = jnp.transpose(o) * (1.0 / total)
    for i in range(4):
        put(dsend.at[i], 32, o_t[32 * i : 32 * i + 32], lse)

    pl.semaphore_wait(barrier, len(partners))

    kv_copies = []
    for i, (dx, dc) in enumerate(plane):
        j = 2 * dx + dc
        h = lax.rem(c + dc, 2)
        kcol = pl.multiple_of(h * D, D)
        vcol = pl.multiple_of(2 * D + h * D, D)
        blk = blk_at(dx, 0, dc)
        for n, (src, dst) in enumerate([
            (pc.at[:, pl.ds(kcol, D)], kbuf.at[pl.ds(j * ROWS, ROWS)]),
            (pc.at[:, pl.ds(vcol, D)], vbuf.at[pl.ds(j * ROWS, ROWS)]),
            (new.at[:, pl.ds(kcol, D)], kbuf.at[pl.ds(4 * ROWS + j * TOK, TOK)]),
            (new.at[:, pl.ds(vcol, D)], vbuf.at[pl.ds(4 * ROWS + j * TOK, TOK)]),
        ]):
            cp = rcopy(src, dst, s_kv.at[4 * i + n], r_kv.at[4 * i + n], blk, r)
            cp.start()
            kv_copies.append(cp)
    q_copies = {}
    order = []
    for k in range(1, Z // 2 + 1):
        order.append(k)
        if Z - k != k:
            order.append(Z - k)
    for k in order + [0]:
        for dc in range(2):
            if k == 0 and dc == 0:
                continue
            half = pl.multiple_of(lax.rem(c + dc, 2) * 4 * D, 4 * D)
            cp = rcopy(
                q.at[:, pl.ds(half, 4 * D)], qall.at[k, dc],
                s_q.at[2 * k + dc], r_q.at[2 * k + dc], blk_at(0, k, dc), r,
            )
            cp.start()
            q_copies[k, dc] = cp
    my_plane = xh * 2 + c
    d1_copies = []
    for i, (dx, dc) in enumerate(plane):
        to = lax.rem(xh + dx, 2) * 2 + lax.rem(c + dc, 2)
        cp = rcopy(dsend.at[to], d1.at[i], s_d1.at[i], r_d1.at[i], blk_at(dx, 0, dc), r)
        cp.start()
        d1_copies.append(cp)

    kcol = pl.multiple_of(c * D, D)
    vcol = pl.multiple_of(2 * D + c * D, D)
    half = pl.multiple_of(c * 4 * D, 4 * D)
    own = []
    for n, (src, dst) in enumerate([
        (pc.at[:, pl.ds(kcol, D)], kbuf.at[pl.ds(0, ROWS)]),
        (pc.at[:, pl.ds(vcol, D)], vbuf.at[pl.ds(0, ROWS)]),
        (new.at[:, pl.ds(kcol, D)], kbuf.at[pl.ds(4 * ROWS, TOK)]),
        (new.at[:, pl.ds(vcol, D)], vbuf.at[pl.ds(4 * ROWS, TOK)]),
        (q.at[:, pl.ds(half, 4 * D)], qall.at[0, 0]),
    ]):
        cp = pltpu.make_async_copy(src, dst, s_loc.at[n])
        cp.start()
        own.append(cp)

    offset = off[0]
    for j in range(4):
        blk = blk_at(j // 2, 0, j % 2)
        at = blk * ROWS + iota((ROWS, 128), 0)
        keyval[j * ROWS : (j + 1) * ROWS, :] = jnp.where(at < offset, at, BIG)
        keyval[4 * ROWS + j * TOK : 4 * ROWS + (j + 1) * TOK, :] = (
            offset + blk * TOK + iota((TOK, 128), 0)
        )

    for cp in d1_copies:
        cp.wait_recv()
    part, lse = merge([dsend.at[my_plane]] + [d1.at[i] for i in range(3)], 32)
    put(d3.at[0], 32, part, lse)
    d3_copies = []
    for k in order:
        cp = rcopy(d3.at[0], d3.at[k], s_d3.at[k], r_d3.at[k], blk_at(0, k, 0), r)
        cp.start()
        d3_copies.append(cp)

    for cp in own:
        cp.wait()
    for cp in kv_copies:
        cp.wait_recv()
    v_t = jnp.transpose(vbuf[...].astype(F32)).astype(BF)
    lane_core = lax.rem(lane // TOK, 2)
    lane_tok = lax.rem(lane, TOK)
    p_copies = {}
    for k in order + [0]:
        for dc in range(2):
            if (k, dc) in q_copies:
                q_copies[k, dc].wait_recv()
        qrows = jnp.concatenate(
            [qall[k, dc, :, h * D : (h + 1) * D] for h in range(4) for dc in range(2)], axis=0
        )
        s = dot(kbuf[...], qrows, NT)
        home = xh * (2 * Z) + lax.rem(z + Z - k, Z) * 2
        tok = (home + lax.rem(c + lane_core, 2)) * TOK + lane_tok
        p, total, lse = soft(jnp.where(keyval[...] <= offset + tok, s, NEG))
        o_t = jnp.dot(v_t, p.astype(BF), preferred_element_type=F32)
        if k == 0:
            put(pall.at[0], D, o_t * (1.0 / total), lse)
        else:
            put(psend.at[k], D, o_t * (1.0 / total), lse)
            cp = rcopy(psend.at[k], pall.at[k], s_p.at[k], r_p.at[k], blk_at(0, Z - k, 0), r)
            cp.start()
            p_copies[k] = cp

    n_copies = []
    for k in order:
        for n, (src, dst) in enumerate([
            (kbuf.at[pl.ds(4 * ROWS, 4 * TOK)], nk.at[pl.ds(k * 4 * TOK, 4 * TOK)]),
            (vbuf.at[pl.ds(4 * ROWS, 4 * TOK)], nv.at[pl.ds(k * 4 * TOK, 4 * TOK)]),
        ]):
            cp = rcopy(src, dst, s_n.at[2 * k + n], r_n.at[2 * k + n], blk_at(0, k, 0), r)
            cp.start()
            n_copies.append(cp)
    nk[0 : 4 * TOK, :] = kbuf[4 * ROWS : 4 * ROWS + 4 * TOK, :]
    nv[0 : 4 * TOK, :] = vbuf[4 * ROWS : 4 * ROWS + 4 * TOK, :]

    for cp in d3_copies:
        cp.wait_recv()
    part, lse = merge([d3.at[k] for k in range(Z)], 32)
    rdq[0] = part.astype(BF)
    rd_copies = []
    for i, (dy, dl) in enumerate(reqs):
        if i:
            cp = rcopy(rdq.at[0], rdq.at[i], s_rd.at[i], r_rd.at[i], b, req_at(dy, dl))
            cp.start()
            rd_copies.append(cp)

    for k in order:
        p_copies[k].wait_recv()
    part, lse = merge([pall.at[k] for k in range(Z)], D)
    att = jnp.transpose(part).astype(BF)
    for dc in range(2):
        for h in range(4):
            lo = h * 2 * TOK + dc * TOK
            rsend[dc, :, h * D : (h + 1) * D] = att[lo : lo + TOK, :]
    r_copies = []
    for i, (dy, dl) in enumerate(reqs):
        for dc in range(2):
            if i or dc:
                cp = rcopy(
                    rsend.at[dc], rall.at[i, dc], s_r.at[2 * i + dc], r_r.at[2 * i + dc],
                    blk_at(0, 0, dc), req_at(dy, dl),
                )
                cp.start()
                r_copies.append(cp)

    for cp in rd_copies:
        cp.wait_recv()
    target = r * SLOTS + lax.rem(iota((128, 128), 0), SLOTS)
    same_head = iota((128, 128), 0) // SLOTS == iota((128, 128), 1) // SLOTS
    picked = jnp.zeros((32, 128), F32)
    for i, (dy, dl) in enumerate(reqs):
        source = req_at(Y - dy, dl)
        dealt = jnp.zeros((1, 128), I32)
        for j in range(SLOTS):
            dealt = jnp.where(lane_slot == j, deal[NP + source * SLOTS + j], dealt)
        chosen = jnp.where(same_head & (target == dealt), 1.0, 0.0).astype(BF)
        picked = picked + dot(rdq[i], chosen, NT)
    df[my_plane] = picked.astype(BF)
    df_copies = []
    for i, (dx, dc) in enumerate(plane):
        cp = rcopy(
            df.at[my_plane], df.at[my_plane], s_df.at[i], r_df.at[i], blk_at(dx, 0, dc), r
        )
        cp.start()
        df_copies.append(cp)

    for cp in n_copies:
        cp.wait_recv()
    width = Z * 4 * TOK
    col = iota((1, width), 1)
    ck = col // (4 * TOK)
    cj = lax.rem(col // TOK, 4)
    cblk = (
        lax.rem(xh + cj // 2, 2) * (2 * Z)
        + lax.rem(z + Z - ck, Z) * 2
        + lax.rem(c + lax.rem(cj, 2), 2)
    )
    tok_of = offset + cblk * TOK + lax.rem(col, TOK)
    partner = blk_at(0, 0, 1)
    picks = []
    for blk in (b, partner):
        hot = jnp.where(blk * ROWS + iota((ROWS, width), 0) == tok_of, 1.0, 0.0).astype(BF)
        picks.append((
            jnp.dot(hot, nk[...], preferred_element_type=F32).astype(BF),
            jnp.dot(hot, nv[...], preferred_element_type=F32).astype(BF),
        ))
    sel[0] = picks[1][0]
    sel[1] = picks[1][1]
    nx_copy = rcopy(sel, nx, s_nx.at[0], r_nx.at[0], partner, r)
    nx_copy.start()

    for cp in r_copies:
        cp.wait_recv()
    for dc in range(2):
        acc = rsend[0] if dc == 0 else rall[0, 1]
        for i, (dy, dl) in enumerate(reqs):
            if i:
                acc = jnp.where(deal[req_at(Y - dy, dl)] == r, rall[i, dc], acc)
        half = pl.multiple_of(lax.rem(c + dc, 2) * 4 * D, 4 * D)
        pout[:, pl.ds(half, 4 * D)] = acc
    for cp in df_copies:
        cp.wait_recv()
    full = jnp.transpose(df[...].reshape(128, 128).astype(F32)).astype(BF)
    for h in range(HEADS):
        dout[:, h * D : (h + 1) * D] = full[h * SLOTS : (h + 1) * SLOTS, :]
    nx_copy.wait_recv()
    at = b * ROWS + iota((ROWS, D), 0)
    inside = (at >= offset) & (at < offset + 2 * 2 * Z * TOK)
    for n in range(2):
        own_col = pl.multiple_of(2 * n * D + c * D, D)
        other_col = pl.multiple_of(2 * n * D + lax.rem(c + 1, 2) * D, D)
        cout[:, pl.ds(own_col, D)] = jnp.where(inside, picks[0][n], pc[:, pl.ds(own_col, D)])
        cout[:, pl.ds(other_col, D)] = jnp.where(inside, nx[n], pc[:, pl.ds(other_col, D)])

    for group in (
        kv_copies, list(q_copies.values()), d1_copies, d3_copies, list(p_copies.values()),
        n_copies, rd_copies, r_copies, df_copies, [nx_copy],
    ):
        for cp in group:
            cp.wait_send()


def make_kernel(Z, Y):
    NR = 2 * Y
    vm = pl.BlockSpec(memory_space=pltpu.VMEM)
    sm = pl.BlockSpec(memory_space=pltpu.SMEM)
    dma = lambda n: pltpu.SemaphoreType.DMA((n,))
    scratch = [
        pltpu.VMEM((4 * ROWS + 4 * TOK, D), BF),
        pltpu.VMEM((4 * ROWS + 4 * TOK, D), BF),
        pltpu.VMEM((4 * ROWS + 4 * TOK, 128), I32),
        pltpu.VMEM((Z, 2, TOK, 4 * D), BF),
        pltpu.VMEM((SLOTS, ROWS, 4 * D), BF),
        pltpu.VMEM((4, 48, 128), BF),
        pltpu.VMEM((3, 48, 128), BF),
        pltpu.VMEM((Z, 48, 128), BF),
        pltpu.VMEM((NR, 32, 128), BF),
        pltpu.VMEM((4, 32, 128), BF),
        pltpu.VMEM((Z, 144, 128), BF),
        pltpu.VMEM((Z, 144, 128), BF),
        pltpu.VMEM((Z * 4 * TOK, D), BF),
        pltpu.VMEM((Z * 4 * TOK, D), BF),
        pltpu.VMEM((2, ROWS, D), BF),
        pltpu.VMEM((2, ROWS, D), BF),
        pltpu.VMEM((2, TOK, 4 * D), BF),
        pltpu.VMEM((NR, 2, TOK, 4 * D), BF),
        dma(4), dma(5),
        dma(12), dma(12), dma(2 * Z), dma(2 * Z), dma(Z), dma(Z), dma(2 * Z), dma(2 * Z),
        dma(3), dma(3), dma(Z), dma(Z), dma(NR), dma(NR), dma(3), dma(3), dma(1), dma(1),
        dma(2 * NR), dma(2 * NR),
    ]
    return pl.pallas_call(
        functools.partial(body, Z, Y),
        out_shape=(
            jax.ShapeDtypeStruct((TOK, HEADS * D), BF),
            jax.ShapeDtypeStruct((SLOTS, HEADS * D), BF),
            jax.ShapeDtypeStruct((ROWS, 4 * D), BF),
        ),
        in_specs=[vm, vm, vm, vm, pl.BlockSpec(memory_space=pl.ANY), sm, sm, sm],
        out_specs=(vm, vm, vm),
        scratch_shapes=scratch,
        compiler_params=pltpu.CompilerParams(
            collective_id=0, has_side_effects=True, vmem_limit_bytes=48 * 1024 * 1024
        ),
    )


def per_device(
    Z, Y, prefill_queries, decode_queries, new_prefill, new_decode, prefill_cache, decode_cache,
    prefill_offsets, decode_lengths, dealing,
):
    positions = lax.axis_index("blk") * ROWS + jnp.arange(ROWS, dtype=I32)
    written = positions[None, :] == decode_lengths[:, None]
    decode_cache_out = jnp.where(written[:, :, None], new_decode[:, None, :], decode_cache)
    prefill_out, decode_out, prefill_cache_out = make_kernel(Z, Y)(
        prefill_queries[0], decode_queries, new_prefill[0], prefill_cache[0], decode_cache_out,
        prefill_offsets, decode_lengths, dealing,
    )
    return prefill_out[None], decode_out, prefill_cache_out[None], decode_cache_out


def solution(mesh):
    Z, Y = mesh.shape["blk"] // 4, mesh.shape["req"] // 2
    in_specs = (
        P("req", "blk", None), P("req", None), P("req", "blk", None), P("req", None),
        P("req", "blk", None), P("req", "blk", None), P("req"), P("req"), P(),
    )
    out_specs = (
        P("req", "blk", None), P("req", None), P("req", "blk", None), P("req", "blk", None),
    )
    return jax.shard_map(
        functools.partial(per_device, Z, Y), mesh=mesh, in_specs=in_specs, out_specs=out_specs,
        check_vma=False,
    )
```
